32 devices in a mesh: groups: 1, epouter: 16 (over z, y, core), epinner: 2 (over x).
Axes of the slice: x: 2, y: 2, z: 4, core: 2. Of those that a mesh axis runs over, the one named last changes fastest.
Arguments:
- tokens: bfloat16 [1024, 7168], P(('groups', 'epouter'), 'epinner'), may hold values from -6 to 6
- expert_ids: int32 [1024, 2], P(('groups', 'epouter')), may hold values from 0 to 3, all different within a row; in each aligned block of 64 rows (0 to 63, 64 to 127, ...) at most 48 rows name the same one
- route_weight: float32 [1024, 2], P(('groups', 'epouter')), may hold values from 0.1 to 0.5
- w_gate: bfloat16 [16, 7168, 384], P('epouter', 'epinner'), may hold values from -0.0625 to 0.0625
- w_up: bfloat16 [16, 7168, 384], P('epouter', 'epinner'), may hold values from -0.0625 to 0.0625
- w_down: bfloat16 [16, 384, 7168], P('epouter', None, 'epinner'), may hold values from -0.15625 to 0.15625
Outputs:
- moe_out: bfloat16 [1024, 7168], P(('groups', 'epouter'), 'epinner')
The draws below stay inside these ranges and needn't reach their ends.
Inputs may be any that keep to these rules, and one draw needn't show every extreme that they name: `expert_ids`: each row names 2 different experts; in each aligned block of 64 rows (the rows of one index of epouter) no expert is named by more than 48 rows, and in some block one expert is named by exactly 48 rows.
All inputs are finite; a program needn't handle non-finite values.
Results may differ from the reference program's by a relative error of at most 0.0058.
Values may be sent and summed in bfloat16 or wider, within the bound.
No kernel may reach another device: no remote copies, remote signals or barrier semaphores. Data moves between devices by JAX's collectives and lax.ppermute only.
A program may use at most 64 MiB of HBM per device.

```python
import math
import jax
import jax.numpy as jnp
import numpy as np
from jax import lax

D = 7168
MOE_HID = 1536
SLICES = 4
HID_DEV = 384
BLOCK = 64
EXPERTS = 4
TOP = 2
CAP = 48
TOKENS = 1024
N_EPOUTER = 16


def levels(key, shape, shards, low, largest):
    def one(axis_at, parts):
        draws = jax.random.uniform(jax.random.fold_in(jax.random.fold_in(key, 6), axis_at), (parts,), jnp.float32, low / len(shards), largest / len(shards))
        return jnp.repeat(jnp.exp(draws), shape[axis_at] // parts).reshape((-1,) + (1,) * (len(shape) - axis_at - 1))

    gain = one(*shards[0])
    for cut in shards[1:]:
        gain = gain * one(*cut)
    return gain


def routed_block(rng, own, number, rows, number_of, top, most, slope):
    ranking = jax.random.permutation(rng, number_of)
    packed, ordinary = portions_of(number_of, rows * top, most, slope, True), portions_of(number_of, rows * top, most, slope, False)
    places = jnp.arange(number_of)

    def named(tallies, offset_by):
        used = int((tallies > 0).sum())
        fixed = max(1, used // 4)
        passed = fixed + (places - fixed + offset_by * (used - fixed)) % max(1, number_of - fixed)
        return jnp.zeros((number_of,), jnp.int32).at[ranking[jnp.where(places < fixed, places, passed)]].set(jnp.asarray(tallies, jnp.int32))

    tallies = jnp.where(number % 4 == 0, named(packed, number // 4), named(ordinary, number - number // 4 - 1))
    mixed = jax.random.permutation(jax.random.fold_in(own, 3), number_of)
    source_of, taker = mixed[0:number_of // 2 * 2:2], mixed[1:number_of // 2 * 2:2]
    slack = jnp.minimum(tallies[source_of] - 1, most - tallies[taker]) // 2
    slack = jnp.where((source_of == ranking[0]) | (taker == ranking[0]) | (tallies[taker] == 0), 0, jnp.maximum(slack, 0))
    passed = jax.random.randint(jax.random.fold_in(own, 4), (number_of // 2,), 0, 1 << 20) % (slack + 1)
    tallies = tallies.at[source_of].add(-passed).at[taker].add(passed)
    members = jnp.searchsorted(jnp.cumsum(tallies), jnp.arange(rows * top), side="right").astype(jnp.int32)
    table = members.reshape(top, rows).T
    table = table[jax.random.permutation(jax.random.fold_in(own, 1), rows)]
    offset_by = jax.random.randint(jax.random.fold_in(own, 2), (rows, 1), 0, top)
    return jnp.take_along_axis(table, (jnp.arange(top)[None, :] + offset_by) % top, axis=1)


def portions_of(number_of, total, reach, lean, full):
    loads = [(1 << 20) // math.isqrt(standing ** lean) + 1 for standing in range(1, number_of + 1)]
    largest = reach if full else min(reach, max(-(-total // number_of), total * loads[0] // sum(loads)))
    least = 1 if total - largest >= number_of - 1 else 0
    holding, spare = [largest] + [least] * (number_of - 1), total - largest - least * (number_of - 1)
    while spare > 0:
        movable = [i for i in range(1, number_of) if holding[i] < largest] or [i for i in range(1, number_of) if holding[i] < reach]
        mass, left = sum([loads[i] for i in movable]), spare
        for i in movable:
            extra = min(reach - holding[i], max(1, left * loads[i] // mass), spare)
            holding[i] = holding[i] + extra
            spare = spare - extra
    return np.array(holding)


def centred(own_key, dims, width, bound, cuts=(), kind=jnp.bfloat16):
    factor_of = levels(own_key, dims, cuts, -0.22, 0.18) if cuts else 1.0
    array = jax.random.normal(own_key, dims, jnp.float32) * width * factor_of
    return jnp.minimum(jnp.maximum(array, -bound), bound).astype(kind)


def setup_inputs(seed: int = 0, part: int = 0) -> dict:
    seeds = jax.random.split(jax.random.key(seed), 7)
    part_keys = jax.random.split(jax.random.fold_in(seeds[6], part), 7)
    tokens = centred(part_keys[0], (TOKENS, D), 1.0, 6.0, ((0, 16), (1, 2)))
    expert_ids_keys = jax.random.split(jax.random.fold_in(part_keys[1], 1), TOKENS // BLOCK)
    expert_ids_turns = jax.random.permutation(jax.random.fold_in(part_keys[1], 3), TOKENS // BLOCK)
    expert_ids = jax.vmap(lambda own, number: routed_block(jax.random.fold_in(part_keys[1], 2), own, number, BLOCK, EXPERTS, TOP, CAP, 2))(expert_ids_keys, expert_ids_turns).reshape((TOKENS, TOP))
    route_weight = jnp.clip(0.1 + 0.4 * jax.random.uniform(part_keys[2], (TOKENS, TOP), jnp.float32) ** levels(part_keys[2], (TOKENS, TOP), ((0, 16),), -0.2, 0.2), 0.1, 0.5)
    w_gate = centred(seeds[3], (EXPERTS * SLICES, D, HID_DEV), D ** -0.5, 0.0625, ((0, 16), (1, 2)))
    w_up = centred(seeds[4], (EXPERTS * SLICES, D, HID_DEV), D ** -0.5, 0.0625, ((0, 16), (1, 2)))
    w_down = centred(seeds[5], (EXPERTS * SLICES, HID_DEV, D), MOE_HID ** -0.5, 0.15625, ((0, 16), (2, 2)))
    return {"tokens": tokens, "expert_ids": expert_ids, "route_weight": route_weight, "w_gate": w_gate, "w_up": w_up, "w_down": w_down}


def reference(tokens, expert_ids, route_weight, w_gate, w_up, w_down):
    experts = w_gate.shape[0] // SLICES
    limit = min(tokens.shape[0], N_EPOUTER * CAP)

    def add_expert(total, expert):
        coefficient = jnp.sum(jnp.where(expert_ids == expert, route_weight, 0.0), axis=1)
        chosen = jnp.sum((expert_ids == expert).astype(jnp.int32), axis=1)
        order = jnp.argsort(-chosen, stable=True)[:limit].astype(jnp.int32)
        rows = jnp.take(tokens, order, axis=0)
        expert_sum = jnp.zeros((limit, tokens.shape[1]), jnp.float32)
        for slice_index in range(SLICES):
            weight_index = (expert * SLICES + slice_index).astype(jnp.int32)
            gate_matrix = lax.dynamic_index_in_dim(w_gate, weight_index, 0, keepdims=False)
            up_matrix = lax.dynamic_index_in_dim(w_up, weight_index, 0, keepdims=False)
            down_matrix = lax.dynamic_index_in_dim(w_down, weight_index, 0, keepdims=False)
            gate_part = jnp.dot(rows, gate_matrix, preferred_element_type=jnp.float32)
            up_part = jnp.dot(rows, up_matrix, preferred_element_type=jnp.float32)
            hidden = (jax.nn.silu(gate_part) * up_part).astype(jnp.bfloat16)
            part_out = jnp.dot(hidden, down_matrix, preferred_element_type=jnp.float32).astype(jnp.bfloat16)
            expert_sum = expert_sum + part_out.astype(jnp.float32)
        scaled = jnp.take(coefficient, order, axis=0)[:, None] * expert_sum
        return total.at[order].add(scaled), None

    start = jnp.zeros(tokens.shape, jnp.float32)
    total, unused = lax.scan(add_expert, start, jnp.arange(experts, dtype=jnp.int32))
    return total.astype(jnp.bfloat16)
```

```python
import jax
import jax.numpy as jnp
from jax import lax
from jax.sharding import PartitionSpec as P

SLICES = 4


def exchange(value, axis, flip):
    size = lax.axis_size(axis)
    return lax.ppermute(value, axis, [(i, i ^ flip) for i in range(size)])


def routes(expert_ids, expert, depth):
    named = jnp.any(expert_ids == expert, axis=1)
    slot = jnp.cumsum(named.astype(jnp.int32)) - 1
    slots = jnp.arange(depth, dtype=jnp.int32)[:, None]
    return (slot[None, :] == slots) & named[None, :]


def shards(tokens, expert_ids, route_weight, w_gate, w_up, w_down):
    outer = lax.axis_size("epouter")
    inner = lax.axis_size("epinner")
    experts = outer // SLICES
    block = tokens.shape[0]
    picks = expert_ids.shape[1]
    depth = min(block, 3 * block * picks // (2 * experts))
    depth = -(-depth // 16) * 16
    mine = lax.axis_index("epouter") // SLICES
    gate_matrix, up_matrix, down_matrix = w_gate[0], w_up[0], w_down[0]

    selections = [routes(expert_ids, mine ^ j, depth) for j in range(experts)]
    chosen = jnp.concatenate(selections, axis=0).astype(jnp.bfloat16)
    packed = jnp.dot(chosen, tokens, preferred_element_type=jnp.float32).astype(jnp.bfloat16)
    packed = packed.reshape(experts, depth, -1)

    total = jnp.zeros(tokens.shape, jnp.float32)
    for j in range(experts):
        own = packed[j]
        if j:
            own = exchange(own, "epouter", SLICES * j)
        across = exchange(own, "epouter", 2)
        pair = jnp.concatenate([own, across], axis=0)
        other = exchange(pair, "epouter", 1)
        rows = jnp.concatenate([pair, other], axis=0)
        gate = jnp.dot(rows, gate_matrix, preferred_element_type=jnp.float32)
        up = jnp.dot(rows, up_matrix, preferred_element_type=jnp.float32)
        sent = jnp.stack([gate.astype(jnp.bfloat16), up.astype(jnp.bfloat16)])
        for k in range(1, inner):
            came = exchange(sent, "epinner", k).astype(jnp.float32)
            gate, up = gate + came[0], up + came[1]
        hidden = (jax.nn.silu(gate) * up).astype(jnp.bfloat16)
        out = jnp.dot(hidden, down_matrix, preferred_element_type=jnp.float32)
        half = out[: 2 * depth] + exchange(
            out[2 * depth :].astype(jnp.bfloat16), "epouter", 1
        ).astype(jnp.float32)
        part = half[:depth] + exchange(
            half[depth:].astype(jnp.bfloat16), "epouter", 2
        ).astype(jnp.float32)
        result = part.astype(jnp.bfloat16)
        if j:
            result = exchange(result, "epouter", SLICES * j)
        weight = jnp.sum(jnp.where(expert_ids == (mine ^ j), route_weight, 0.0), axis=1)
        fetched = jnp.dot(
            selections[j].astype(jnp.bfloat16).T, result, preferred_element_type=jnp.float32
        )
        total = total + weight[:, None] * fetched
    return total.astype(jnp.bfloat16)


def solution(mesh):
    placed = (
        P(("groups", "epouter"), "epinner"),
        P(("groups", "epouter"), None),
        P(("groups", "epouter"), None),
        P("epouter", "epinner", None),
        P("epouter", "epinner", None),
        P("epouter", None, "epinner"),
    )
    return jax.shard_map(
        shards,
        mesh=mesh,
        in_specs=placed,
        out_specs=P(("groups", "epouter"), "epinner"),
        check_vma=False,
    )
```
